512 devices in a mesh: trans: 64 (over x, z, core), bin: 8 (over y).
Axes of the slice: x: 4, y: 8, z: 8, core: 2. Of those that a mesh axis runs over, the one named last changes fastest.
Arguments:
- pair_density: bfloat16 [32768, 8000], P('trans', 'bin'), may hold values from -1.5 to 1.5
- bin_index: int32 [32768, 1], P('trans'), may hold values from 0 to 255; in each aligned block of 512 rows (0 to 511, 512 to 1023, ...) at most 4 rows name the same one
- panel_columns: int32 [128], replicated, may hold values from 0 to 7999
Outputs:
- response: float32 [2, 256, 1024000], P(None, None, ('bin', 'trans'))
The draws below stay inside these ranges and needn't reach their ends.
Inputs may be any that keep to these rules, and one draw needn't show every extreme that they name: `bin_index`: among the 512 transitions of one device no bin occurs more than 4 times, and some bin occurs exactly 4 times. `panel_columns`: entries may repeat.
All inputs are finite; a program needn't handle non-finite values.
Results may differ from the reference program's by a relative error of at most 0.0003.
Values may be sent and summed in bfloat16 or wider, within the bound.
A program may use at most 64 MiB of HBM per device.

```python
import math
import jax
import jax.numpy as jnp
import numpy as np
from jax import lax

G = 8000
PANEL = 128
NB = 256
MOST = 4
TRANS_DEV = 512
TRANS = 32768
N_TRANS = 64
N_BIN = 8


def set_ends(drawn, own_key, least, largest):
    spot = [jax.random.randint(jax.random.fold_in(own_key, axis), (), 0, length) for axis, length in enumerate(drawn.shape)]
    widest = drawn.shape.index(max(drawn.shape))
    beside = spot[:widest] + [(spot[widest] + 1) % drawn.shape[widest]] + spot[widest + 1:]
    return drawn.at[tuple(spot)].set(least).at[tuple(beside)].set(largest)


def levels(stream_key, dims, pieces, smallest, high):
    def one(axis_at, blocks):
        draws = jax.random.uniform(jax.random.fold_in(jax.random.fold_in(stream_key, 6), axis_at), (blocks,), jnp.float32, smallest / len(pieces), high / len(pieces))
        return jnp.repeat(jnp.exp(draws), dims[axis_at] // blocks).reshape((-1,) + (1,) * (len(dims) - axis_at - 1))

    level = one(*pieces[0])
    for cut in pieces[1:]:
        level = level * one(*cut)
    return level


def assign_block(key, own, number, rows, amount, top, limit, lean):
    sequence = jax.random.permutation(key, amount)
    crowded, usual = shares(amount, rows * top, limit, lean, True), shares(amount, rows * top, limit, lean, False)
    places = jnp.arange(amount)

    def named(sizes, turn):
        used = int((sizes > 0).sum())
        fixed = max(1, used // 4)
        passed = fixed + (places - fixed + turn * (used - fixed)) % max(1, amount - fixed)
        return jnp.zeros((amount,), jnp.int32).at[sequence[jnp.where(places < fixed, places, passed)]].set(jnp.asarray(sizes, jnp.int32))

    sizes = jnp.where(number % 4 == 0, named(crowded, number // 4), named(usual, number - number // 4 - 1))
    mixed = jax.random.permutation(jax.random.fold_in(own, 3), amount)
    giver, taker = mixed[0:amount // 2 * 2:2], mixed[1:amount // 2 * 2:2]
    room = jnp.minimum(sizes[giver] - 1, limit - sizes[taker]) // 2
    room = jnp.where((giver == sequence[0]) | (taker == sequence[0]) | (sizes[taker] == 0), 0, jnp.maximum(room, 0))
    passed = jax.random.randint(jax.random.fold_in(own, 4), (amount // 2,), 0, 1 << 20) % (room + 1)
    sizes = sizes.at[giver].add(-passed).at[taker].add(passed)
    members = jnp.searchsorted(jnp.cumsum(sizes), jnp.arange(rows * top), side="right").astype(jnp.int32)
    grid = members.reshape(top, rows).T
    grid = grid[jax.random.permutation(jax.random.fold_in(own, 1), rows)]
    turn = jax.random.randint(jax.random.fold_in(own, 2), (rows, 1), 0, top)
    return jnp.take_along_axis(grid, (jnp.arange(top)[None, :] + turn) % top, axis=1)


def shares(count, total, bound, skew, full):
    weights = [(1 << 20) // math.isqrt(rank ** skew) + 1 for rank in range(1, count + 1)]
    largest = bound if full else min(bound, max(-(-total // count), total * weights[0] // sum(weights)))
    least = 1 if total - largest >= count - 1 else 0
    holding, rest = [largest] + [least] * (count - 1), total - largest - least * (count - 1)
    while rest > 0:
        candidates = [i for i in range(1, count) if holding[i] < largest] or [i for i in range(1, count) if holding[i] < bound]
        pool, budget = sum([weights[i] for i in candidates]), rest
        for i in candidates:
            extra = min(bound - holding[i], max(1, budget * weights[i] // pool), rest)
            holding[i] = holding[i] + extra
            rest = rest - extra
    return np.array(holding)


def bell_draw(rng, shape, deviation, limit, pieces=(), held_as=jnp.bfloat16):
    drawn = deviation * jax.random.normal(rng, shape, jnp.float32)
    if pieces:
        drawn = drawn * levels(rng, shape, pieces, -0.22, 0.18)
    return jnp.clip(drawn, -limit, limit).astype(held_as)


def setup_inputs(seed: int = 0) -> dict:
    arg_keys = jax.random.split(jax.random.key(seed), 4)
    pair_density = bell_draw(arg_keys[0], (TRANS, G), 0.25, 1.5, ((0, 64), (1, 8)))
    bin_index_keys = jax.random.split(jax.random.fold_in(arg_keys[1], 1), TRANS // TRANS_DEV)
    bin_index_turns = jax.random.permutation(jax.random.fold_in(arg_keys[1], 3), TRANS // TRANS_DEV)
    bin_index = jax.vmap(lambda own, number: assign_block(jax.random.fold_in(arg_keys[1], 2), own, number, TRANS_DEV, NB, 1, MOST, 2))(bin_index_keys, bin_index_turns).reshape((TRANS, 1))
    panel_columns = set_ends(jax.random.randint(arg_keys[2], (PANEL,), 0, G), jax.random.fold_in(arg_keys[2], 1), 0, G - 1).astype(jnp.int32)
    return {"pair_density": pair_density, "bin_index": bin_index, "panel_columns": panel_columns}


broaden = 1.5


def kernel_tables():
    freq = jnp.arange(NB, dtype=jnp.int32).astype(jnp.float32) + 0.5
    diff = freq[:, None] - freq[None, :]
    total = freq[:, None] + freq[None, :]
    low = diff * diff + broaden * broaden
    high = total * total + broaden * broaden
    return diff / low - total / high, broaden / high - broaden / low


def reference(pair_density, bin_index, panel_columns):
    bin_number = bin_index[:, 0]
    order = jnp.argsort(bin_number, stable=True)
    counts = jnp.sum((bin_number[:, None] == jnp.arange(NB, dtype=jnp.int32)[None, :]).astype(jnp.int32), axis=0).astype(jnp.int32)
    starts = (jnp.cumsum(counts) - counts).astype(jnp.int32)
    window = N_TRANS * MOST
    panel = pair_density[:, panel_columns]
    rows_sorted = jnp.concatenate([pair_density[order], jnp.zeros((window, G), pair_density.dtype)], axis=0)
    panel_sorted = jnp.concatenate([panel[order], jnp.zeros((window, PANEL), panel.dtype)], axis=0).astype(jnp.float32)
    row_count = G // N_BIN
    kernel_re, kernel_im = kernel_tables()

    def one_block(index):
        rows = lax.dynamic_slice_in_dim(rows_sorted, (index * row_count).astype(jnp.int32), row_count, 1)

        def one_bin(which):
            start = starts[which]
            chosen = lax.dynamic_slice_in_dim(rows, start, window, 0).astype(jnp.float32)
            paired = lax.dynamic_slice_in_dim(panel_sorted, start, window, 0)
            live = (jnp.arange(window, dtype=jnp.int32) < counts[which]).astype(jnp.float32)
            return jnp.dot((chosen * live[:, None]).T, paired, precision=lax.Precision.HIGHEST, preferred_element_type=jnp.float32)

        spectral = lax.map(one_bin, jnp.arange(NB, dtype=jnp.int32))
        flat = spectral.reshape(NB, row_count * PANEL)
        real_part = jnp.dot(kernel_re, flat, precision=lax.Precision.HIGHEST, preferred_element_type=jnp.float32)
        imag_part = jnp.dot(kernel_im, flat, precision=lax.Precision.HIGHEST, preferred_element_type=jnp.float32)
        return jnp.stack([real_part, imag_part])

    blocks = lax.map(one_block, jnp.arange(N_BIN, dtype=jnp.int32))
    return jnp.transpose(blocks, (1, 2, 0, 3)).reshape(2, NB, G * PANEL)
```

```python
import functools

import jax
import jax.numpy as jnp
from jax import lax
from jax.experimental import pallas as pl
from jax.experimental.pallas import tpu as pltpu
from jax.sharding import PartitionSpec as P

PANEL = 128
NB = 256
BROADEN = 1.5
ZN, XN, YN = 8, 4, 8
NT = 64
QUARTERS = 4
WINDOW = 18
MSG = WINDOW * QUARTERS
HALF = 32
PD_EARLY = 16
MESH = pl.DeviceIdType.MESH
BF16 = jnp.bfloat16
F32 = jnp.float32


def window_pair(owner):
    return jnp.minimum((owner * 125 // 8) // 2, 491)


def exchange_kernel(pd, part, bins, y_out, bin_out, buf_a, buf_b, slots, piece, *sems):
    (pd_s, pd_r, bn_s, bn_r, loc, y0_s, y0_r, za_s, za_r, zb_s, zb_r, xa_s, xa_r, ra_s, ra_r, rb_s, rb_r,
     rx_s, rx_r, ca_s, ca_r, cb_s, cb_r) = sems
    t, y = lax.axis_index("trans"), lax.axis_index("bin")
    core, chip = lax.rem(t, 2), t // 2
    x, z = chip // ZN, lax.rem(chip, ZN)

    barrier = pltpu.get_barrier_semaphore()

    def greet(k, carry):
        pl.semaphore_signal(barrier, inc=1, device_id=(lax.rem(t + k, NT), y), device_id_type=MESH)
        return carry

    def greet_y(k, carry):
        pl.semaphore_signal(barrier, inc=1, device_id=(t, lax.rem(y + k, YN)), device_id_type=MESH)
        return carry

    lax.fori_loop(1, NT, greet, 0)
    lax.fori_loop(1, YN, greet_y, 0)
    pl.semaphore_wait(barrier, NT - 1 + YN - 1)

    def remote(src, dst, send, recv, device):
        return pltpu.make_async_remote_copy(
            src_ref=src, dst_ref=dst, send_sem=send, recv_sem=recv, device_id=device, device_id_type=MESH
        )

    sent = []

    def go(copy):
        copy.start()
        sent.append(copy)
        return copy

    def rows(start, size):
        return pl.ds(pl.multiple_of(start, 8), size)

    for k in range(1, YN):
        to = lax.rem(y + k, YN)
        go(remote(part.at[rows(to * 64, 64)], slots.at[y], y0_s.at[k], y0_r.at[k], (t, to)))
    own = pltpu.make_async_copy(part.at[rows(y * 64, 64)], slots.at[y], loc.at[0])
    own.start()

    def pd_copy(k, to, frm):
        return remote(
            pd.at[rows(window_pair(to) * 8, MSG)], y_out.at[rows(frm * MSG, MSG)], pd_s.at[k], pd_r.at[k], (to, y)
        )

    def bin_copy(k, to, frm):
        return remote(bins, bin_out.at[rows(frm * 8, 8)], bn_s.at[k], bn_r.at[k], (to, y))

    def pd_start(k, carry):
        to = lax.rem(t + k, NT)
        pd_copy(k, to, t).start()
        bin_copy(k, to, t).start()
        return carry

    lax.fori_loop(1, PD_EARLY, pd_start, 0)
    own_pd = pltpu.make_async_copy(pd.at[rows(window_pair(t) * 8, MSG)], y_out.at[rows(t * MSG, MSG)], loc.at[1])
    own_pd.start()
    own_bin = pltpu.make_async_copy(bins, bin_out.at[rows(t * 8, 8)], loc.at[2])
    own_bin.start()

    own.wait()
    for k in range(1, YN):
        frm = lax.rem(y - k + YN, YN)
        remote(part.at[rows(0, 64)], slots.at[frm], y0_s.at[k], y0_r.at[k], (t, frm)).wait_recv()
    total = slots[0].astype(F32)
    for k in range(1, YN):
        total = total + slots[k].astype(F32)
    piece[...] = total.astype(BF16)

    a_own = buf_a.at[core * YN + y, rows(chip * HALF, HALF)]
    b_own = buf_b.at[core * XN + x, rows((y * ZN + z) * HALF, HALF)]
    pa, pb = piece.at[rows(0, HALF)], piece.at[rows(HALF, HALF)]
    la = pltpu.make_async_copy(pa, a_own, loc.at[3])
    lb = pltpu.make_async_copy(pb, b_own, loc.at[4])
    la.start()
    lb.start()
    for k in range(1, ZN):
        to = (x * ZN + lax.rem(z + k, ZN)) * 2 + core
        go(remote(pb, b_own, zb_s.at[k], zb_r.at[k], (to, y)))
        go(remote(pa, a_own, za_s.at[k], za_r.at[k], (to, y)))
    la.wait()
    lb.wait()
    for k in range(1, ZN):
        zf = lax.rem(z - k + ZN, ZN)
        frm = (x * ZN + zf) * 2 + core
        b_dst = buf_b.at[core * XN + x, rows((y * ZN + zf) * HALF, HALF)]
        a_dst = buf_a.at[core * YN + y, rows((x * ZN + zf) * HALF, HALF)]
        remote(pb, b_dst, zb_s.at[k], zb_r.at[k], (frm, y)).wait_recv()
        remote(pa, a_dst, za_s.at[k], za_r.at[k], (frm, y)).wait_recv()

    y_right, y_left = lax.rem(y + 1, YN), lax.rem(y + YN - 1, YN)

    def b_part(yy, half=None):
        base, size = lax.rem(yy + 2 * YN, YN) * (ZN * HALF), ZN * HALF
        if half is not None:
            base, size = base + half * (size // 2), size // 2
        return buf_b.at[core * XN + x, rows(base, size)]

    def a_part(yy, half=None):
        lead = core * YN + lax.rem(yy + 2 * YN, YN)
        if half is None:
            return buf_a.at[lead]
        return buf_a.at[lead, rows(half * 512, 512)]

    def x_part(xx, half=None):
        lead = core * XN + lax.rem(xx + 2 * XN, XN)
        if half is None:
            return buf_b.at[lead]
        return buf_b.at[lead, rows(half * 1024, 1024)]

    def ring_send(part_of, me, s, last, send, recv, right, left):
        h = s == last
        r_ref = part_of(me - s, 0 if h else None)
        l_ref = part_of(me + s, 1 if h else None)
        go(remote(r_ref, r_ref, send.at[0, s], recv.at[0, s], right))
        go(remote(l_ref, l_ref, send.at[1, s], recv.at[1, s], left))

    def ring_wait(part_of, me, s, last, send, recv, right, left):
        h = s == last
        r_ref = part_of(me - 1 - s, 0 if h else None)
        l_ref = part_of(me + 1 + s, 1 if h else None)
        remote(r_ref, r_ref, send.at[0, s], recv.at[0, s], left).wait_recv()
        remote(l_ref, l_ref, send.at[1, s], recv.at[1, s], right).wait_recv()

    ring_b = (b_part, y, rb_s, rb_r, (t, y_right), (t, y_left))
    ring_a = (a_part, y, ra_s, ra_r, (t, y_right), (t, y_left))
    xr = (lax.rem(x + 1, XN) * ZN + z) * 2 + core
    xl = (lax.rem(x + XN - 1, XN) * ZN + z) * 2 + core
    ring_x = (x_part, x, rx_s, rx_r, (xr, y), (xl, y))

    def send(ring, s, last):
        ring_send(ring[0], ring[1], s, last, *ring[2:])

    def wait(ring, s, last):
        ring_wait(ring[0], ring[1], s, last, *ring[2:])

    mate = t + 1 - 2 * core

    def pass_a(r):
        ref = a_part(y + r)
        go(remote(ref, ref, ca_s.at[r % YN], ca_r.at[r % YN], (mate, y)))

    def pass_b(r):
        ref = x_part(x + r)
        go(remote(ref, ref, cb_s.at[r % XN], cb_r.at[r % XN], (mate, y)))

    send(ring_b, 0, 3)
    for k in range(1, XN):
        to = (lax.rem(x + k, XN) * ZN + z) * 2 + core
        ref = buf_a.at[core * YN + y, rows(x * (ZN * HALF), ZN * HALF)]
        go(remote(ref, ref, xa_s.at[k], xa_r.at[k], (to, y)))
    lax.fori_loop(PD_EARLY, NT, pd_start, 0)
    for k in range(1, XN):
        xf = lax.rem(x - k + XN, XN)
        frm = (xf * ZN + z) * 2 + core
        ref = buf_a.at[core * YN + y, rows(xf * (ZN * HALF), ZN * HALF)]
        remote(ref, ref, xa_s.at[k], xa_r.at[k], (frm, y)).wait_recv()
    send(ring_a, 0, 3)
    pass_a(0)
    for s in range(3):
        wait(ring_b, s, 3)
        send(ring_b, s + 1, 3)
    wait(ring_b, 3, 3)
    send(ring_x, 0, 1)
    pass_b(0)
    for s in range(3):
        wait(ring_a, s, 3)
        send(ring_a, s + 1, 3)
        pass_a(-1 - s)
        pass_a(1 + s)
    wait(ring_x, 0, 1)
    send(ring_x, 1, 1)
    pass_b(-1)
    pass_b(1)
    wait(ring_a, 3, 3)
    pass_a(4)
    wait(ring_x, 1, 1)
    pass_b(2)

    own_pd.wait()
    own_bin.wait()

    def pd_wait(k, carry):
        frm = lax.rem(t - k + NT, NT)
        pd_copy(k, frm, frm).wait()
        bin_copy(k, frm, frm).wait()
        return carry

    lax.fori_loop(1, NT, pd_wait, 0)
    for copy in sent:
        copy.wait_send()
    for r in range(YN):
        ref = buf_a.at[(1 - core) * YN + lax.rem(y + r, YN)]
        remote(ref, ref, ca_s.at[r], ca_r.at[r], (mate, y)).wait_recv()
    for r in range(XN):
        ref = buf_b.at[(1 - core) * XN + lax.rem(x + r, XN)]
        remote(ref, ref, cb_s.at[r], cb_r.at[r], (mate, y)).wait_recv()


def exchange(pd, part, bins):
    dma = pltpu.SemaphoreType.DMA
    anyspace = pl.BlockSpec(memory_space=pl.ANY)
    return pl.pallas_call(
        exchange_kernel,
        out_shape=(
            jax.ShapeDtypeStruct((NT * MSG, 128), BF16),
            jax.ShapeDtypeStruct((NT * 8, 128), BF16),
            jax.ShapeDtypeStruct((2 * YN, XN * ZN * HALF, PANEL), BF16),
            jax.ShapeDtypeStruct((2 * XN, YN * ZN * HALF, PANEL), BF16),
        ),
        in_specs=[anyspace] * 3,
        out_specs=(anyspace,) * 4,
        scratch_shapes=[
            pltpu.VMEM((YN, 64, PANEL), BF16),
            pltpu.VMEM((64, PANEL), BF16),
            dma((NT,)), dma((NT,)), dma((NT,)), dma((NT,)), dma((5,)),
            dma((YN,)), dma((YN,)),
            dma((ZN,)), dma((ZN,)), dma((ZN,)), dma((ZN,)),
            dma((XN,)), dma((XN,)),
            dma((2, 4)), dma((2, 4)), dma((2, 4)), dma((2, 4)), dma((2, 2)), dma((2, 2)),
            dma((YN,)), dma((YN,)), dma((XN,)), dma((XN,)),
        ],
        compiler_params=pltpu.CompilerParams(collective_id=1, has_side_effects=True),
        name="exchange",
    )(pd, part, bins)


GROUPS = 8
KC = 16
ROWS = WINDOW * 16


def spectral_kernel(y_ref, bin_ref, a_ref, b_ref, table, o_ref, yf, key, par, lhs, rhs, acc, shi, slo, kh, kl):
    t = lax.axis_index("trans")
    first = 125 * t // 8
    shift = lax.rem(80 * t, 128)
    skip = first - 2 * window_pair(t)

    yf[...] = y_ref[...].astype(F32)
    bins = bin_ref[...].astype(F32)
    group = jnp.floor(bins * (1 / 32))
    inner = bins - group * 32
    parity = jnp.floor(inner * (1 / 16))
    key[...] = group * 16 + (inner - parity * 16)
    par[...] = parity
    acc[...] = jnp.zeros_like(acc)
    line = lax.broadcasted_iota(jnp.int32, (NT * 8, 128), 0) % 8
    low = lax.broadcasted_iota(jnp.int32, (16, 128), 0).astype(F32)

    def quarter(q, carry):
        here = line == q
        g_lo = jnp.min(jnp.where(here, group, 1e3)).astype(jnp.int32)
        g_hi = jnp.max(jnp.where(here, group, -1.0)).astype(jnp.int32)

        def build(chip, c2):
            x, z = chip // ZN, lax.rem(chip, ZN)
            for core in range(2):
                src = chip * 2 + core
                odd = jnp.broadcast_to(par[pl.ds(src * 8 + q, 1), :], (128, 128)).T.astype(BF16)
                pieces = []
                for i in range(2):
                    yy = 2 * q + i
                    pieces.append(a_ref[core * YN + yy, pl.ds(pl.multiple_of(chip * HALF, HALF), HALF), :])
                    pieces.append(
                        b_ref[core * XN + x, pl.ds(pl.multiple_of((yy * ZN + z) * HALF, HALF), HALF), :]
                    )
                block = jnp.concatenate(pieces, axis=0)
                high = block * odd
                at = pl.ds(pl.multiple_of(src * 128, 128), 128)
                rhs[at, 128:256] = high
                rhs[at, 0:128] = block - high
            return c2

        lax.fori_loop(0, NT // 2, build, 0)

        def one_group(g, c2):
            want = low + (g * 16).astype(F32)

            def chunk(k, c3):
                for i in range(KC):
                    src = k * KC + i
                    mask = jnp.broadcast_to(key[pl.ds(src * 8 + q, 1), :], (16, 128)) == want
                    for w in range(WINDOW):
                        row = jnp.broadcast_to(yf[pl.ds(src * MSG + w * QUARTERS + q, 1), :], (16, 128))
                        lhs[w * 16:(w + 1) * 16, i * 128:(i + 1) * 128] = jnp.where(mask, row, 0.0).astype(BF16)
                at = pl.ds(pl.multiple_of(k * (KC * 128), 128), KC * 128)
                acc[g, 0:ROWS, :] += jnp.dot(lhs[...], rhs[at, :], preferred_element_type=F32)
                return c3

            return lax.fori_loop(0, NT // KC, chunk, c2)

        return lax.fori_loop(g_lo, g_hi + 1, one_group, carry)

    lax.fori_loop(0, QUARTERS, quarter, 0)

    lane = lax.broadcasted_iota(jnp.int32, (16, 128), 1)

    def align(k, carry):
        for g in range(GROUPS):
            for p in range(2):
                cols = slice(p * 128, (p + 1) * 128)
                this = acc[g, pl.ds(pl.multiple_of((skip + k) * 16, 16), 16), cols]
                after = acc[g, pl.ds(pl.multiple_of((skip + k + 1) * 16, 16), 16), cols]
                turned = pltpu.roll(jnp.where(lane < shift, after, this), lax.rem(128 - shift, 128), 1)
                hi = turned.astype(BF16)
                at = pl.ds(pl.multiple_of(k * 128, 128), 128)
                r0 = g * 32 + p * 16
                shi[r0:r0 + 16, at] = hi
                slo[r0:r0 + 16, at] = (turned - hi.astype(F32)).astype(BF16)
        return carry

    lax.fori_loop(0, 16, align, 0)
    dot = functools.partial(jnp.dot, preferred_element_type=F32)
    kh[...] = table[...].astype(BF16)
    kl[...] = (table[...] - kh[...].astype(F32)).astype(BF16)
    for n in range(4):
        width = min(512, 2000 - n * 512)
        at = slice(n * 512, n * 512 + 512)
        part = dot(kh[...], shi[:, at]) + dot(kh[...], slo[:, at]) + dot(kl[...], shi[:, at])
        o_ref[:, n * 512:n * 512 + width] = part[:, :width]


def spectral_response(y_in, bins, a, b, table):
    vm = pl.BlockSpec(memory_space=pltpu.VMEM)
    return pl.pallas_call(
        spectral_kernel,
        out_shape=jax.ShapeDtypeStruct((2 * NB, 2000), F32),
        in_specs=[vm] * 5,
        out_specs=vm,
        scratch_shapes=[
            pltpu.VMEM((NT * MSG, 128), F32),
            pltpu.VMEM((NT * 8, 128), F32),
            pltpu.VMEM((NT * 8, 128), F32),
            pltpu.VMEM((ROWS, KC * 128), BF16),
            pltpu.VMEM((NT * 128, 256), BF16),
            pltpu.VMEM((GROUPS, ROWS + 16, 256), F32),
            pltpu.VMEM((NB, 2048), BF16),
            pltpu.VMEM((NB, 2048), BF16),
            pltpu.VMEM((2 * NB, NB), BF16),
            pltpu.VMEM((2 * NB, NB), BF16),
        ],
        compiler_params=pltpu.CompilerParams(vmem_limit_bytes=60 << 20),
        name="spectral",
    )(y_in, bins, a, b, table)


def kernel_table():
    freq = lax.broadcasted_iota(jnp.int32, (NB, 1), 0).astype(F32) + 0.5
    diff = freq - freq[:, 0][None, :]
    total = freq + freq[:, 0][None, :]
    low = diff * diff + BROADEN * BROADEN
    high = total * total + BROADEN * BROADEN
    return jnp.concatenate([diff / low - total / high, BROADEN / high - BROADEN / low], axis=0)


def local(pair_density, bin_index, panel_columns):
    count, width = pair_density.shape
    place = lax.axis_index("bin")
    bin_number = bin_index[:, 0]
    key = bin_number * count + lax.iota(jnp.int32, count)
    position = jnp.sum((key[None, :] < key[:, None]).astype(jnp.int32), axis=1)
    sorting = lax.broadcasted_iota(jnp.int32, (count, count), 0) == position[None, :]
    perm = sorting.astype(BF16)
    ordered = jnp.sum(jnp.where(sorting, bin_number[None, :], 0), axis=1)
    bins = jnp.pad(ordered.astype(BF16).reshape(QUARTERS, 128), ((0, 4), (0, 0)))
    selector = (
        lax.broadcasted_iota(jnp.int32, (width, PANEL), 0) + place * width == panel_columns[None, :]
    ).astype(BF16)
    turned = lax.dot_general(
        pair_density, perm, (((0,), (1,)), ((), ())), preferred_element_type=F32
    ).astype(BF16)
    part = jnp.dot(pair_density, selector, preferred_element_type=F32).astype(BF16)
    part = jnp.dot(perm, part, preferred_element_type=F32).astype(BF16)
    y_in, all_bins, a, b = exchange(turned.reshape(width * QUARTERS, 128), part, bins)
    return spectral_response(y_in, all_bins, a, b, kernel_table()).reshape(2, NB, 2000)


def solution(mesh):
    placed = (P("trans", "bin"), P("trans", None), P())
    return jax.shard_map(
        local,
        mesh=mesh,
        in_specs=placed,
        out_specs=P(None, None, ("bin", "trans")),
        check_vma=False,
    )
```
